32 devices in a mesh: section: 2 (over y), dp: 4 (over x, core), expert: 4 (over z).
Axes of the slice: x: 2, y: 2, z: 4, core: 2. Of those that a mesh axis runs over, the one named last changes fastest.
Arguments:
- upstream: bfloat16 [2, 256, 4096], P('section', 'expert', 'dp'), may hold values from -6 to 6
- routes: int32 [2, 256, 2], P('section', 'expert'), may hold values from 0 to 3, all different within a row; in each aligned block of 64 rows (0 to 63, 64 to 127, ..., all dimensions but the last counted through in order) at most 48 rows name the same one
- gate_weights: bfloat16 [2, 256, 2], P('section', 'expert'), may hold values from 0.049804688 to 0.5
- w_gate: bfloat16 [2, 4, 4096, 768], P('section', 'expert', 'dp'), may hold values from -0.09375 to 0.09375
- w_up: bfloat16 [2, 4, 4096, 768], P('section', 'expert', 'dp'), may hold values from -0.09375 to 0.09375
- w_down: bfloat16 [2, 4, 768, 4096], P('section', 'expert', None, 'dp'), may hold values from -0.21875 to 0.21875
- saved_gate: bfloat16 [2, 4, 4, 48, 768], P('section', 'expert'), may hold values from -6 to 6
- saved_up: bfloat16 [2, 4, 4, 48, 768], P('section', 'expert'), may hold values from -6 to 6
Outputs:
- handed: bfloat16 [2, 256, 4096], P('section', 'expert', 'dp')
- gate_grads: bfloat16 [2, 256, 2], P('section', 'expert')
The draws below stay inside these ranges and needn't reach their ends.
Inputs may be any that keep to these rules, and one draw needn't show every extreme that they name: `routes`: each token names 2 different experts; among the 64 tokens of one device no expert is named by more than 48 tokens, and in every draw some expert is named by exactly 48 tokens of some device.
All inputs are finite; a program needn't handle non-finite values.
Results may differ from the reference program's by a relative error of at most 0.015.
Values may be sent and summed in bfloat16 or wider, within the bound.
No kernel may reach another device: no remote copies, remote signals or barrier semaphores. Data moves between devices by JAX's collectives and lax.ppermute only.
A program may use at most 64 MiB of HBM per device.

```python
import math
import jax
import jax.numpy as jnp
import numpy as np
from jax import lax

D = 4096
HID = 768
TOK_DEV = 64
EXPERTS = 4
TOP = 2
CAP = 48
TOKENS = 256
N_SECTION = 2
N_DP = 4
N_EXPERT = 4


def block_scale(own_key, extent, cuts, low, top_value):
    level, own = 1.0, jax.random.fold_in(own_key, 6)
    for position, blocks in cuts:
        heights = jnp.exp(jax.random.uniform(jax.random.fold_in(own, position), (blocks,), jnp.float32, low / len(cuts), top_value / len(cuts)))
        level = level * jnp.repeat(heights, extent[position] // blocks).reshape([-1 if axis == position else 1 for axis in range(len(extent))])
    return level


def deal_out(stream_key, own, number, rows, count, top, bound, lean):
    order = jax.random.permutation(stream_key, count)
    crowded, ordinary = portions_of(count, rows * top, bound, lean, True), portions_of(count, rows * top, bound, lean, False)
    places = jnp.arange(count)

    def named(tallies, rotation):
        used = int((tallies > 0).sum())
        fixed = max(1, used // 4)
        moved = fixed + (places - fixed + rotation * (used - fixed)) % max(1, count - fixed)
        return jnp.zeros((count,), jnp.int32).at[order[jnp.where(places < fixed, places, moved)]].set(jnp.asarray(tallies, jnp.int32))

    tallies = jnp.where(number % 4 == 0, named(crowded, number // 4), named(ordinary, number - number // 4 - 1))
    mixed = jax.random.permutation(jax.random.fold_in(own, 3), count)
    donor, sink = mixed[0:count // 2 * 2:2], mixed[1:count // 2 * 2:2]
    slack = jnp.minimum(tallies[donor] - 1, bound - tallies[sink]) // 2
    slack = jnp.where((donor == order[0]) | (sink == order[0]) | (tallies[sink] == 0), 0, jnp.maximum(slack, 0))
    moved = jax.random.randint(jax.random.fold_in(own, 4), (count // 2,), 0, 1 << 20) % (slack + 1)
    tallies = tallies.at[donor].add(-moved).at[sink].add(moved)
    items = jnp.searchsorted(jnp.cumsum(tallies), jnp.arange(rows * top), side="right").astype(jnp.int32)
    table = items.reshape(top, rows).T
    table = table[jax.random.permutation(jax.random.fold_in(own, 1), rows)]
    rotation = jax.random.randint(jax.random.fold_in(own, 2), (rows, 1), 0, top)
    return jnp.take_along_axis(table, (jnp.arange(top)[None, :] + rotation) % top, axis=1)


def portions_of(amount, total, bound, lean, full):
    weights = [(1 << 20) // math.isqrt(standing ** lean) + 1 for standing in range(1, amount + 1)]
    largest = bound if full else min(bound, max(-(-total // amount), total * weights[0] // sum(weights)))
    least = 1 if total - largest >= amount - 1 else 0
    holding, surplus = [largest] + [least] * (amount - 1), total - largest - least * (amount - 1)
    while surplus > 0:
        free = [i for i in range(1, amount) if holding[i] < largest] or [i for i in range(1, amount) if holding[i] < bound]
        whole, left = sum([weights[i] for i in free]), surplus
        for i in free:
            extra = min(bound - holding[i], max(1, left * weights[i] // whole), surplus)
            holding[i] = holding[i] + extra
            surplus = surplus - extra
    return np.array(holding)


def normal_values(own_key, dims, scale, bound, cuts=(), held_as=jnp.bfloat16):
    drawn = scale * jax.random.normal(own_key, dims, jnp.float32)
    if cuts:
        drawn = drawn * block_scale(own_key, dims, cuts, -0.22, 0.18)
    return jnp.clip(drawn, -bound, bound).astype(held_as)


def setup_inputs(seed: int = 0) -> dict:
    arg_keys = jax.random.split(jax.random.key(seed), 9)
    upstream = normal_values(arg_keys[0], (N_SECTION, TOKENS, D), 1.0, 6.0, ((0, 2), (1, 4), (2, 4)))
    routes_keys = jax.random.split(jax.random.fold_in(arg_keys[1], 1), N_SECTION * TOKENS // TOK_DEV)
    routes_turns = jax.random.permutation(jax.random.fold_in(arg_keys[1], 3), N_SECTION * TOKENS // TOK_DEV)
    routes = jax.vmap(lambda own, number: deal_out(jax.random.fold_in(arg_keys[1], 2), own, number, TOK_DEV, EXPERTS, TOP, CAP, 2))(routes_keys, routes_turns).reshape((N_SECTION, TOKENS, TOP))
    gate_weights = jnp.clip(0.049804688 + 0.4501953 * jax.random.uniform(arg_keys[2], (N_SECTION, TOKENS, TOP), jnp.float32) ** block_scale(arg_keys[2], (N_SECTION, TOKENS, TOP), ((0, 2), (1, 4)), -0.2, 0.2), 0.049804688, 0.5).astype(jnp.bfloat16)
    w_gate = normal_values(arg_keys[3], (N_SECTION, EXPERTS, D, HID), D ** -0.5, 0.09375, ((0, 2), (1, 4), (2, 4)))
    w_up = normal_values(arg_keys[4], (N_SECTION, EXPERTS, D, HID), D ** -0.5, 0.09375, ((0, 2), (1, 4), (2, 4)))
    w_down = normal_values(arg_keys[5], (N_SECTION, EXPERTS, HID, D), HID ** -0.5, 0.21875, ((0, 2), (1, 4), (3, 4)))
    saved_gate = normal_values(arg_keys[6], (N_SECTION, EXPERTS, N_EXPERT, CAP, HID), 1.0, 6.0, ((0, 2), (1, 4)))
    saved_up = normal_values(arg_keys[7], (N_SECTION, EXPERTS, N_EXPERT, CAP, HID), 1.0, 6.0, ((0, 2), (1, 4)))
    return {"upstream": upstream, "routes": routes, "gate_weights": gate_weights, "w_gate": w_gate, "w_up": w_up, "w_down": w_down, "saved_gate": saved_gate, "saved_up": saved_up}


def block_slots(route_block):
    labels = jnp.arange(EXPERTS, dtype=jnp.int32)
    onehot = (route_block[:, :, None] == labels[None, None, :]).astype(jnp.int32)
    per_token = jnp.sum(onehot, axis=1)
    earlier = jnp.cumsum(per_token, axis=0) - per_token
    return jnp.sum(onehot * earlier[:, None, :], axis=2).astype(jnp.int32)


def split_sum(values):
    rounded = lax.optimization_barrier(values.astype(jnp.bfloat16))
    return jnp.sum(rounded.astype(jnp.float32), axis=0)


def expert_pass(packed):
    slot_rows, slot_gate, w_gate_e, w_up_e, w_down_e, gate_pre, up_pre = packed
    row_count = slot_rows.shape[0]
    scaled = (slot_gate.astype(jnp.float32)[:, None] * slot_rows.astype(jnp.float32)).astype(jnp.bfloat16)
    pieces = jnp.einsum("rnd,hnd->nrh", scaled.astype(jnp.float32).reshape(row_count, N_DP, D // N_DP),
                        w_down_e.astype(jnp.float32).reshape(HID, N_DP, D // N_DP))
    hidden_grad = split_sum(pieces)
    gate_val = gate_pre.astype(jnp.float32)
    up_val = up_pre.astype(jnp.float32)
    sigmoid_val = jax.nn.sigmoid(gate_val)
    silu_val = gate_val * sigmoid_val
    hidden = (silu_val * up_val).astype(jnp.bfloat16)
    gate_back = (hidden_grad * up_val * sigmoid_val * (1.0 + gate_val * (1.0 - sigmoid_val))).astype(jnp.bfloat16)
    up_back = (hidden_grad * silu_val).astype(jnp.bfloat16)
    expert_out = jnp.dot(hidden, w_down_e, preferred_element_type=jnp.float32).astype(jnp.bfloat16)
    inner_terms = jnp.sum((expert_out.astype(jnp.float32) * slot_rows.astype(jnp.float32)).reshape(row_count, N_DP, D // N_DP), axis=2)
    slot_grad = split_sum(inner_terms.T).astype(jnp.bfloat16)
    row_grad = (jnp.dot(gate_back, w_gate_e.T, preferred_element_type=jnp.float32)
                + jnp.dot(up_back, w_up_e.T, preferred_element_type=jnp.float32)).astype(jnp.bfloat16)
    return row_grad, slot_grad


def section_pass(upstream_s, routes_s, gates_s, w_gate_s, w_up_s, w_down_s, saved_gate_s, saved_up_s):
    blocks = routes_s.reshape(N_EXPERT, TOK_DEV, TOP)
    slot = jax.vmap(block_slots)(blocks).reshape(TOKENS, TOP)
    source = (jnp.arange(TOKENS, dtype=jnp.int32) // TOK_DEV)[:, None]
    target = ((routes_s.astype(jnp.int32) * N_EXPERT + source) * CAP + slot).astype(jnp.int32)
    total_slots = EXPERTS * N_EXPERT * CAP
    pair_ids = jnp.arange(TOKENS * TOP, dtype=jnp.int32)
    holder = jnp.zeros((total_slots,), jnp.int32).at[target.reshape(-1)].set(pair_ids + 1)
    filled = holder > 0
    pair_index = jnp.maximum(holder - 1, 0).astype(jnp.int32)
    zero_value = jnp.zeros((), jnp.bfloat16)
    slot_rows = jnp.where(filled[:, None], upstream_s[pair_index // TOP], zero_value)
    slot_gate = jnp.where(filled, gates_s.reshape(-1)[pair_index], zero_value)
    rows_each = N_EXPERT * CAP
    row_grad, slot_grad = lax.map(expert_pass, (
        slot_rows.reshape(EXPERTS, rows_each, D),
        slot_gate.reshape(EXPERTS, rows_each),
        w_gate_s, w_up_s, w_down_s,
        saved_gate_s.reshape(EXPERTS, rows_each, HID),
        saved_up_s.reshape(EXPERTS, rows_each, HID)))
    row_grad = row_grad.reshape(total_slots, D)
    slot_grad = slot_grad.reshape(total_slots)
    routed_sum = jnp.zeros((TOKENS, D), jnp.float32)
    for pick in range(TOP):
        routed_sum = routed_sum + row_grad[target[:, pick]].astype(jnp.float32)
    layer_grad = (upstream_s.astype(jnp.float32) + routed_sum).astype(jnp.bfloat16)
    gate_grads = slot_grad[target]
    return layer_grad, gate_grads


def reference(upstream, routes, gate_weights, w_gate, w_up, w_down, saved_gate, saved_up):
    layer_list = []
    grad_list = []
    for section_index in range(N_SECTION):
        layer_grad, gate_grads = section_pass(upstream[section_index], routes[section_index], gate_weights[section_index],
                                            w_gate[section_index], w_up[section_index], w_down[section_index],
                                            saved_gate[section_index], saved_up[section_index])
        layer_list.append(layer_grad)
        grad_list.append(gate_grads)
    handed = jnp.stack(layer_list[1:] + [jnp.zeros_like(layer_list[0])])
    return handed, jnp.stack(grad_list)
```

```python
import jax
import jax.numpy as jnp
from jax import lax
from jax.sharding import PartitionSpec as P

AXES = ("section", "dp", "expert")
TRANSPOSED = (((1,), (1,)), ((), ()))


def device_pairs(route):
    sections, parts, experts = (lax.axis_size(name) for name in AXES)
    pairs = []
    for section in range(sections):
        for part in range(parts):
            for expert in range(experts):
                target = route(section, part, expert)
                if target is not None:
                    source_id = (section * parts + part) * experts + expert
                    target_id = (target[0] * parts + target[1]) * experts + target[2]
                    pairs.append((source_id, target_id))
    return pairs


def moved(value, route):
    return lax.ppermute(value, AXES, device_pairs(route))


def matmul(lhs, rhs):
    return jnp.dot(lhs, rhs, preferred_element_type=jnp.float32)


def matmul_t(lhs, rhs):
    return lax.dot_general(lhs, rhs, TRANSPOSED, preferred_element_type=jnp.float32)


def per_device(upstream, routes, gate_weights, w_gate, w_up, w_down, saved_gate, saved_up):
    grads_here = upstream[0]
    route_block = routes[0]
    gates_here = gate_weights[0].astype(jnp.float32)
    parts = lax.axis_size("dp")
    experts = lax.axis_size("expert")
    capacity = saved_gate.shape[3]
    tokens, picks = route_block.shape
    steps = experts // 2
    expert_id = lax.axis_index("expert")
    core = lax.axis_index("dp") & 1

    place = jnp.arange(experts, dtype=jnp.int32)
    labels = expert_id ^ ((place & ~1) + ((place & 1) ^ core))

    named = route_block[:, :, None] == labels[None, None, :]
    names = jnp.any(named, axis=1)
    order = jnp.arange(tokens, dtype=jnp.int32)
    before = (order[None, :] < order[:, None]).astype(jnp.bfloat16)
    earlier = matmul(before, names.astype(jnp.bfloat16)).astype(jnp.int32)
    slot = jnp.where(names, earlier, -1)
    gate_of = jnp.sum(jnp.where(named, gates_here[:, :, None], 0.0), axis=1)
    holds = slot[:, :, None] == jnp.arange(capacity, dtype=jnp.int32)[None, None, :]
    placement = holds.reshape(tokens, experts * capacity).astype(jnp.bfloat16)
    gated = (
        jnp.where(holds, gate_of[:, :, None], 0.0)
        .reshape(tokens, experts * capacity)
        .astype(jnp.bfloat16)
    )
    rows = lax.dot_general(
        placement, grads_here, (((0,), (0,)), ((), ())), preferred_element_type=jnp.float32
    ).astype(jnp.bfloat16)

    def row_block(index):
        return rows[index * capacity : (index + 1) * capacity]

    down_own, gate_own, up_own = (w_down[0, 0], w_gate[0, 0], w_up[0, 0])
    partner = lambda s, d, e: (s, d ^ 1, e)
    down_other = moved(down_own, partner)

    same_core = [moved(row_block(2 * j), lambda s, d, e, j=j: (s, d, e ^ (2 * j + (d & 1)))) for j in range(steps)]
    cross_core = [
        moved(row_block(2 * j + 1), lambda s, d, e, j=j: (s, d ^ 1, e ^ (2 * j + 1 - (d & 1))))
        for j in range(steps)
    ]
    gate_other = moved(gate_own, partner)
    up_other = moved(up_own, partner)

    def expert_back(chosen):
        own = jnp.concatenate([same_core[j] for j in chosen])
        other = jnp.concatenate([cross_core[j] for j in chosen])

        def picked(saved):
            return jnp.concatenate(
                [
                    lax.dynamic_index_in_dim(saved[0, 0], expert_id ^ (2 * j + core), 0, False)
                    for j in chosen
                ]
            ).astype(jnp.float32)

        total = (matmul_t(own, down_own) + matmul_t(other, down_other)).astype(jnp.bfloat16)
        distance = 2
        while distance < parts:
            arrived = moved(total, lambda s, d, e, b=distance: (s, d ^ b, e))
            total = total.astype(jnp.float32) + arrived.astype(jnp.float32)
            distance *= 2
            if distance < parts:
                total = total.astype(jnp.bfloat16)
        total = total.astype(jnp.float32)
        gate_val, up_val = picked(saved_gate), picked(saved_up)
        sigmoid_val = jax.nn.sigmoid(gate_val)
        silu_val = gate_val * sigmoid_val
        hidden = (silu_val * up_val).astype(jnp.bfloat16).astype(jnp.float32)
        slot_grad = jnp.sum(hidden * total, axis=1).astype(jnp.bfloat16)
        gate_back = (
            total * up_val * sigmoid_val * (1.0 + gate_val * (1.0 - sigmoid_val))
        ).astype(jnp.bfloat16)
        up_back = (total * silu_val).astype(jnp.bfloat16)
        row_own = (matmul_t(gate_back, gate_own) + matmul_t(up_back, up_own)).astype(jnp.bfloat16)
        row_other = (matmul_t(gate_back, gate_other) + matmul_t(up_back, up_other)).astype(
            jnp.bfloat16
        )
        return (row_own, row_other, slot_grad)

    near = expert_back([0])
    far = expert_back(list(range(1, steps)))

    def part_of(result, which, j):
        if j == 0:
            return near[which]
        return far[which][(j - 1) * capacity : j * capacity]

    def back_same(j, shift):
        return lambda s, d, e: (s - shift, d, e ^ (2 * j + (d & 1))) if s >= shift else None

    def back_cross(j, shift):
        return lambda s, d, e: (s - shift, d ^ 1, e ^ (2 * j + (d & 1))) if s >= shift else None

    only_later = lambda route: (lambda s, d, e: route(s, d, e) if s >= 1 else None)

    near_rows = jnp.concatenate(
        [
            moved(near[0], only_later(back_same(0, 0))),
            moved(near[1], only_later(back_cross(0, 0))),
        ]
    )
    far_rows = []
    for j in range(1, steps):
        far_rows.append(moved(part_of(far, 0, j), back_same(j, 1)))
        far_rows.append(moved(part_of(far, 1, j), back_cross(j, 1)))
    partial = (
        grads_here.astype(jnp.float32) + matmul(gated[:, : 2 * capacity], near_rows)
    ).astype(jnp.bfloat16)
    message = jnp.concatenate([partial, gated[:, 2 * capacity :]], axis=1)
    message = moved(message, lambda s, d, e: (s - 1, d, e) if s >= 1 else None)
    width = grads_here.shape[1]
    handed = message[:, :width].astype(jnp.float32)
    if far_rows:
        handed = handed + matmul(message[:, width:], jnp.concatenate(far_rows))
    handed = handed.astype(jnp.bfloat16)

    slot_back = []
    for j in range(steps):
        slot_back.append(moved(part_of(None, 2, j)[None], back_same(j, 0)))
        slot_back.append(moved(part_of(None, 2, j)[None], back_cross(j, 0)))
    slot_back = jnp.concatenate(slot_back).astype(jnp.float32)
    back_of = jnp.sum(jnp.where(holds, slot_back[None], 0.0), axis=2)
    gate_grads = jnp.sum(jnp.where(named, back_of[:, None, :], 0.0), axis=2).astype(jnp.bfloat16)
    return (handed[None], gate_grads[None])


def solution(mesh):
    placed = (
        P("section", "expert", "dp"),
        P("section", "expert", None),
        P("section", "expert", None),
        P("section", "expert", "dp", None),
        P("section", "expert", "dp", None),
        P("section", "expert", None, "dp"),
        P("section", "expert", None, None, None),
        P("section", "expert", None, None, None),
    )
    return jax.shard_map(
        per_device,
        mesh=mesh,
        in_specs=placed,
        out_specs=(P("section", "expert", "dp"), P("section", "expert", None)),
        check_vma=False,
    )
```

```python
import functools

import jax
import jax.numpy as jnp
from jax import lax
from jax.experimental import pallas as pl
from jax.experimental.pallas import tpu as pltpu
from jax.sharding import PartitionSpec as P


AXES = ("section", "dp", "expert")
TRANSPOSED = (((1,), (1,)), ((), ()))
LEADING = (((0,), (0,)), ((), ()))


def device_pairs(route):
    sections, parts, experts = (lax.axis_size(name) for name in AXES)
    pairs = []
    for section in range(sections):
        for part in range(parts):
            for expert in range(experts):
                target = route(section, part, expert)
                if target is not None:
                    source_id = (section * parts + part) * experts + expert
                    target_id = (target[0] * parts + target[1]) * experts + target[2]
                    pairs.append((source_id, target_id))
    return pairs


def moved(value, route):
    return lax.ppermute(value, AXES, device_pairs(route))


def matmul(lhs, rhs):
    return jnp.dot(lhs, rhs, preferred_element_type=jnp.float32)


def matmul_t(lhs, rhs):
    return lax.dot_general(lhs, rhs, TRANSPOSED, preferred_element_type=jnp.float32)


def kernel_call(body, outs, ins, flops=0, spaces=None, scratch=()):
    spaces = spaces or [pltpu.VMEM] * len(ins)
    ins = [
        pltpu.with_memory_space_constraint(value, space) if space == pltpu.HBM else value
        for value, space in zip(ins, spaces)
    ]
    size = sum(value.size * value.dtype.itemsize for value in ins)
    return pl.pallas_call(
        body,
        out_shape=outs,
        in_specs=[pl.BlockSpec(memory_space=space) for space in spaces],
        out_specs=jax.tree.map(lambda _: pl.BlockSpec(memory_space=pltpu.VMEM), outs),
        scratch_shapes=scratch,
        compiler_params=pltpu.CompilerParams(vmem_limit_bytes=16 * 2**20),
        cost_estimate=pl.CostEstimate(flops=flops, bytes_accessed=size, transcendentals=0),
    )(*ins)


def table_kernel(capacity, experts, expert_ref, route_hbm, gate_hbm, grads_hbm, *refs):
    row_refs, (gated_ref, hold_ref) = (refs[:experts], refs[experts : experts + 2])
    route_ref, gate_ref, grads_ref, semaphores = refs[experts + 2 :]
    copies = [
        pltpu.make_async_copy(source, target, semaphores.at[index])
        for index, (source, target) in enumerate(
            ((route_hbm, route_ref), (gate_hbm, gate_ref), (grads_hbm, grads_ref))
        )
    ]
    for copy in copies:
        copy.start()
    picks, tokens = route_ref.shape
    slots = experts * capacity
    place = lax.broadcasted_iota(jnp.int32, (slots, 1), 0)
    block = lax.div(place, capacity)
    inside = (place - block * capacity).astype(jnp.float32)
    label = expert_ref[0] ^ block
    row = lax.broadcasted_iota(jnp.int32, (tokens, tokens), 0)
    column = lax.broadcasted_iota(jnp.int32, (tokens, tokens), 1)
    before = jnp.where(row < column, 1.0, 0.0).astype(jnp.bfloat16)
    copies[0].wait()
    named = [route_ref[pick : pick + 1, :] == label for pick in range(picks)]
    names = functools.reduce(jnp.logical_or, named)
    earlier = matmul(jnp.where(names, 1.0, 0.0).astype(jnp.bfloat16), before)
    fits = earlier == inside
    placed = jnp.where(names & fits, 1.0, 0.0).astype(jnp.bfloat16)
    copies[2].wait()
    for k, ref in enumerate(row_refs):
        ref[...] = matmul(placed[k * capacity : (k + 1) * capacity], grads_ref[...]).astype(
            jnp.bfloat16
        )
    copies[1].wait()
    gated = jnp.zeros((slots, tokens), jnp.float32)
    for pick in range(picks):
        here = jnp.where(named[pick] & fits, 1.0, 0.0)
        hold_ref[pick] = here.astype(jnp.bfloat16)
        gated = gated + here * gate_ref[pick : pick + 1, :].astype(jnp.float32)
    gated_ref[...] = gated.astype(jnp.bfloat16)


def fetch_kernel(*refs):
    count = len(refs) // 2
    copies = [
        pltpu.make_async_copy(refs[index], refs[count + index], refs[-1].at[index])
        for index in range(count)
    ]
    for copy in copies:
        copy.start()
    for copy in copies:
        copy.wait()


def raw_kernel(*refs):
    row_refs, down_ref, out_ref = (refs[:-2], refs[-2], refs[-1])
    rows = jnp.concatenate([ref[...] for ref in row_refs])
    out_ref[...] = matmul_t(rows, down_ref[...]).astype(jnp.bfloat16)


def back_kernel(offsets, capacity, near, expert_ref, here_ref, other_ref, saved_gate_ref, saved_up_ref, gate_ref, up_ref, *refs):
    total = here_ref[...].astype(jnp.float32) + other_ref[...].astype(jnp.float32)

    def picked(ref):
        return jnp.concatenate([ref[expert_ref[0] ^ k] for k in offsets]).astype(jnp.float32)

    gate_val, up_val = (picked(saved_gate_ref), picked(saved_up_ref))
    sigmoid_val = jax.nn.sigmoid(gate_val)
    silu_val = gate_val * sigmoid_val
    hidden = (silu_val * up_val).astype(jnp.bfloat16).astype(jnp.float32)
    inner = jnp.sum(hidden * total, axis=1, keepdims=True)
    gate_back = (
        total * up_val * sigmoid_val * (1.0 + gate_val * (1.0 - sigmoid_val))
    ).astype(jnp.bfloat16)
    up_back = (total * silu_val).astype(jnp.bfloat16)
    back = (matmul_t(gate_back, gate_ref[...]) + matmul_t(up_back, up_ref[...])).astype(
        jnp.bfloat16
    )
    inner = jnp.broadcast_to(inner, (inner.shape[0], 128)).astype(jnp.bfloat16)
    outs = iter(refs)
    for index, k in enumerate(offsets):
        own = slice(index * capacity, (index + 1) * capacity)
        if near and k:
            joined = next(outs)
            joined[:, : back.shape[1]] = back[own]
            joined[:, back.shape[1] :] = inner[own]
        else:
            next(outs)[...] = back[own]
            next(outs)[...] = inner[own]


def partial_kernel(grads_ref, gated_ref, first_ref, *refs):
    row_refs, message_ref = (refs[:-1], refs[-1])
    tokens, width = grads_ref.shape
    rows = jnp.concatenate([first_ref[...]] + [ref[:, :width] for ref in row_refs])
    near = rows.shape[0]
    partial = grads_ref[...].astype(jnp.float32) + lax.dot_general(
        gated_ref[:near], rows, LEADING, preferred_element_type=jnp.float32
    )
    message_ref[:, :width] = partial.astype(jnp.bfloat16)
    row = lax.broadcasted_iota(jnp.int32, (tokens, tokens), 0)
    column = lax.broadcasted_iota(jnp.int32, (tokens, tokens), 1)
    same = jnp.where(row == column, 1.0, 0.0).astype(jnp.bfloat16)
    message_ref[:, width:] = matmul_t(same, gated_ref[near:]).astype(jnp.bfloat16)


def combine_kernel(message_ref, *refs):
    row_refs, out_ref = (refs[:-1], refs[-1])
    width = out_ref.shape[1]
    rows = jnp.concatenate([ref[...] for ref in row_refs])
    gated = message_ref[:, width:]
    out_ref[...] = (
        message_ref[:, :width].astype(jnp.float32) + matmul(gated, rows)
    ).astype(jnp.bfloat16)


def gates_kernel(hold_ref, *refs):
    slot_refs, out_ref = (refs[:-1], refs[-1])
    slots = jnp.concatenate([ref[:, ref.shape[1] - 128 :] for ref in slot_refs])
    for pick in range(hold_ref.shape[0]):
        found = lax.dot_general(
            slots, hold_ref[pick], LEADING, preferred_element_type=jnp.float32
        )
        out_ref[pick : pick + 1, :] = found[:1].astype(jnp.bfloat16)


def layer(upstream, routes, gate_weights, w_gate, w_up, w_down, saved_gate, saved_up):
    grads_here = upstream[0]
    route_block = routes[0]
    parts = lax.axis_size("dp")
    experts = lax.axis_size("expert")
    capacity = saved_gate.shape[3]
    tokens, picks = route_block.shape
    width = grads_here.shape[1]
    units = w_down.shape[2]
    expert_id = lax.axis_index("expert").astype(jnp.int32)[None]
    bf16 = lambda *shape: jax.ShapeDtypeStruct(shape, jnp.bfloat16)

    *rows, gated, holds = kernel_call(
        functools.partial(table_kernel, capacity, experts),
        (
            *[bf16(capacity, width)] * experts,
            bf16(experts * capacity, tokens),
            bf16(picks, experts * capacity, tokens),
        ),
        (expert_id, route_block.T, gate_weights[0].T, grads_here),
        2 * experts * capacity * tokens * width,
        [pltpu.SMEM] + [pltpu.HBM] * 3,
        (
            pltpu.VMEM((picks, tokens), jnp.int32),
            pltpu.VMEM((picks, tokens), jnp.bfloat16),
            pltpu.VMEM((tokens, width), jnp.bfloat16),
            pltpu.SemaphoreType.DMA((3,)),
        ),
    )

    def across(k, shift=0):
        return lambda s, d, e: (s - shift, d, e ^ k) if s >= shift else None

    half = experts // 2
    far = [k for k in range(half, experts)]
    cut = (len(far) + 1) // 2
    chunks = {"a": far[:cut], "b": far[cut:], "c": list(range(half))}
    arrived = {0: rows[0]}
    for name in ("a", "b", "c"):
        for k in chunks[name]:
            if k:
                arrived[k] = moved(rows[k], across(k))

    held = (w_down[0, 0], w_gate[0, 0], w_up[0, 0], saved_gate[0, 0], saved_up[0, 0])
    down, gate, up, gate_pre, up_pre = kernel_call(
        fetch_kernel,
        tuple(bf16(*value.shape) for value in held),
        held,
        0,
        [pltpu.HBM] * len(held),
        (pltpu.SemaphoreType.DMA((len(held),)),),
    )
    row_grad, slot_grad = ({}, {})
    for name in ("a", "b", "c"):
        chosen = chunks[name]
        count = len(chosen) * capacity
        total = kernel_call(
            raw_kernel,
            bf16(count, units),
            (*[arrived[k] for k in chosen], down),
            2 * count * width * units,
        )
        distance = 1
        while distance < parts:
            other = moved(total, lambda s, d, e, b=distance: (s, d ^ b, e))
            distance *= 2
            if distance < parts:
                total = (total.astype(jnp.float32) + other.astype(jnp.float32)).astype(jnp.bfloat16)
        near = name == "c"
        outs = []
        for k in chosen:
            if near and k:
                outs.append(bf16(capacity, width + 128))
            else:
                outs.extend([bf16(capacity, width), bf16(capacity, 128)])
        results = list(
            kernel_call(
                functools.partial(back_kernel, tuple(chosen), capacity, near),
                tuple(outs),
                (expert_id, total, other, gate_pre, up_pre, gate, up),
                4 * count * width * units,
                [pltpu.SMEM] + [pltpu.VMEM] * 6,
            )
        )
        for k in chosen:
            row_grad[k] = results.pop(0)
            if not (near and k):
                slot_grad[k] = results.pop(0)

    returned = {}
    for name in ("a", "b", "c"):
        for k in chunks[name]:
            if k:
                returned[k] = moved(row_grad[k], across(k, 0 if name == "c" else 1))
    message = kernel_call(
        partial_kernel,
        bf16(tokens, width + half * capacity),
        (grads_here, gated, row_grad[0], *[returned[k] for k in range(1, half)]),
        2 * tokens * width * half * capacity,
    )
    message = moved(message, lambda s, d, e: (s - 1, d, e) if s >= 1 else None)
    handed = kernel_call(
        combine_kernel,
        bf16(tokens, width),
        (message, *[returned[k] for k in far]),
        2 * tokens * width * half * capacity,
    )
    slot_back = [slot_grad[0], *[returned[k] for k in range(1, half)]]
    for k in far:
        slot_back.append(moved(slot_grad[k], across(k)))
    gate_grads = kernel_call(gates_kernel, bf16(picks, tokens), (holds, *slot_back))
    return (handed[None], gate_grads.T[None])


def solution(mesh):
    placed = (
        P("section", "expert", "dp"),
        P("section", "expert", None),
        P("section", "expert", None),
        P("section", "expert", "dp", None),
        P("section", "expert", "dp", None),
        P("section", "expert", None, "dp"),
        P("section", "expert", None, None, None),
        P("section", "expert", None, None, None),
    )
    return jax.shard_map(
        layer,
        mesh=mesh,
        in_specs=placed,
        out_specs=(P("section", "expert", "dp"), P("section", "expert", None)),
        check_vma=False,
    )
```

```python
import functools

import jax
import jax.numpy as jnp
from jax import lax
from jax.experimental import pallas as pl
from jax.experimental.pallas import tpu as pltpu
from jax.sharding import PartitionSpec as P


AXES = ("section", "dp", "expert")
TRANSPOSED = (((1,), (1,)), ((), ()))
LEADING = (((0,), (0,)), ((), ()))


def device_pairs(route):
    sections, parts, experts = (lax.axis_size(name) for name in AXES)
    pairs = []
    for section in range(sections):
        for part in range(parts):
            for expert in range(experts):
                target = route(section, part, expert)
                if target is not None:
                    source_id = (section * parts + part) * experts + expert
                    target_id = (target[0] * parts + target[1]) * experts + target[2]
                    pairs.append((source_id, target_id))
    return pairs


def moved(value, route):
    return lax.ppermute(value, AXES, device_pairs(route))


def matmul(lhs, rhs):
    return jnp.dot(lhs, rhs, preferred_element_type=jnp.float32)


def matmul_t(lhs, rhs):
    return lax.dot_general(lhs, rhs, TRANSPOSED, preferred_element_type=jnp.float32)


def kernel_call(body, outs, ins, flops=0, spaces=None, scratch=()):
    spaces = spaces or [pltpu.VMEM] * len(ins)
    ins = [
        pltpu.with_memory_space_constraint(value, space) if space == pltpu.HBM else value
        for value, space in zip(ins, spaces)
    ]
    size = sum(value.size * value.dtype.itemsize for value in ins)
    return pl.pallas_call(
        body,
        out_shape=outs,
        in_specs=[pl.BlockSpec(memory_space=space) for space in spaces],
        out_specs=jax.tree.map(lambda _: pl.BlockSpec(memory_space=pltpu.VMEM), outs),
        scratch_shapes=scratch,
        compiler_params=pltpu.CompilerParams(vmem_limit_bytes=16 * 2**20),
        cost_estimate=pl.CostEstimate(flops=flops, bytes_accessed=size, transcendentals=0),
    )(*ins)


def table_kernel(capacity, experts, route_hbm, gate_hbm, grads_hbm, *refs):
    row_refs, (gated_ref, hold_ref) = (refs[:experts], refs[experts : experts + 2])
    route_ref, gate_ref, grads_ref, semaphores = refs[experts + 2 :]
    copies = [
        pltpu.make_async_copy(source, target, semaphores.at[index])
        for index, (source, target) in enumerate(
            ((route_hbm, route_ref), (gate_hbm, gate_ref), (grads_hbm, grads_ref))
        )
    ]
    for copy in copies:
        copy.start()
    picks, tokens = route_ref.shape
    slots = experts * capacity
    place = lax.broadcasted_iota(jnp.int32, (slots, 1), 0)
    block = lax.div(place, capacity)
    inside = (place - block * capacity).astype(jnp.float32)
    label = lax.axis_index("expert") ^ block
    row = lax.broadcasted_iota(jnp.int32, (tokens, tokens), 0)
    column = lax.broadcasted_iota(jnp.int32, (tokens, tokens), 1)
    before = jnp.where(row < column, 1.0, 0.0).astype(jnp.bfloat16)
    copies[0].wait()
    named = [route_ref[pick : pick + 1, :] == label for pick in range(picks)]
    names = functools.reduce(jnp.logical_or, named)
    earlier = matmul(jnp.where(names, 1.0, 0.0).astype(jnp.bfloat16), before)
    fits = earlier == inside
    placed = jnp.where(names & fits, 1.0, 0.0).astype(jnp.bfloat16)
    copies[2].wait()
    for k, ref in enumerate(row_refs):
        ref[...] = matmul(placed[k * capacity : (k + 1) * capacity], grads_ref[...]).astype(
            jnp.bfloat16
        )
    copies[1].wait()
    gated = jnp.zeros((slots, tokens), jnp.float32)
    for pick in range(picks):
        here = jnp.where(named[pick] & fits, 1.0, 0.0)
        hold_ref[pick] = here.astype(jnp.bfloat16)
        gated = gated + here * gate_ref[pick : pick + 1, :].astype(jnp.float32)
    gated_ref[...] = gated.astype(jnp.bfloat16)


def fetch_kernel(source_ref, target_ref, semaphore):
    copy = pltpu.make_async_copy(source_ref, target_ref, semaphore)
    copy.start()
    copy.wait()


def raw_kernel(*refs):
    row_refs, down_ref, out_ref = (refs[:-2], refs[-2], refs[-1])
    rows = jnp.concatenate([ref[...] for ref in row_refs])
    out_ref[...] = matmul_t(rows, down_ref[...]).astype(jnp.bfloat16)


def back_kernel(offsets, capacity, name, here_ref, other_ref, saved_gate_ref, saved_up_ref, gate_ref, up_ref, *refs):
    total = here_ref[...].astype(jnp.float32) + other_ref[...].astype(jnp.float32)

    def picked(ref):
        return jnp.concatenate([ref[lax.axis_index("expert") ^ k] for k in offsets]).astype(jnp.float32)

    gate_val, up_val = (picked(saved_gate_ref), picked(saved_up_ref))
    sigmoid_val = jax.nn.sigmoid(gate_val)
    silu_val = gate_val * sigmoid_val
    hidden = (silu_val * up_val).astype(jnp.bfloat16).astype(jnp.float32)
    inner = jnp.sum(hidden * total, axis=1, keepdims=True)
    gate_back = (
        total * up_val * sigmoid_val * (1.0 + gate_val * (1.0 - sigmoid_val))
    ).astype(jnp.bfloat16)
    up_back = (total * silu_val).astype(jnp.bfloat16)
    back = (matmul_t(gate_back, gate_ref[...]) + matmul_t(up_back, up_ref[...])).astype(
        jnp.bfloat16
    )
    inner = jnp.broadcast_to(inner, (inner.shape[0], 128)).astype(jnp.bfloat16)
    count = len(offsets)
    if name == "b":
        earlier, refs = (refs[:count], refs[count:])
        first = (lax.axis_index("dp") & 1) == 0
    outs = iter(refs)
    for index, k in enumerate(offsets):
        own = slice(index * capacity, (index + 1) * capacity)
        if name == "c" and k:
            joined = next(outs)
            joined[:, : back.shape[1]] = back[own]
            joined[:, back.shape[1] :] = inner[own]
        else:
            next(outs)[...] = back[own]
            next(outs)[...] = (
                jnp.where(first, earlier[index][...], inner[own]) if name == "b" else inner[own]
            )


def partial_kernel(grads_ref, gated_ref, first_ref, *refs):
    row_refs, message_ref = (refs[:-1], refs[-1])
    tokens, width = grads_ref.shape
    rows = jnp.concatenate([first_ref[...]] + [ref[:, :width] for ref in row_refs])
    near = rows.shape[0]
    partial = grads_ref[...].astype(jnp.float32) + lax.dot_general(
        gated_ref[:near], rows, LEADING, preferred_element_type=jnp.float32
    )
    message_ref[:, :width] = partial.astype(jnp.bfloat16)
    row = lax.broadcasted_iota(jnp.int32, (tokens, tokens), 0)
    column = lax.broadcasted_iota(jnp.int32, (tokens, tokens), 1)
    same = jnp.where(row == column, 1.0, 0.0).astype(jnp.bfloat16)
    message_ref[:, width:] = matmul_t(same, gated_ref[near:]).astype(jnp.bfloat16)


def finish_kernel(far, message_ref, hold_ref, *refs):
    count = len(far)
    row_refs, slot_refs, (handed_ref, gates_ref) = (refs[:count], refs[count:-2], refs[-2:])
    near_refs, near_slots, other_slots = (
        slot_refs[:-count],
        slot_refs[-count : -(count // 2)],
        slot_refs[-(count // 2) :],
    )
    first = (lax.axis_index("dp") & 1) == 0
    found = {}
    for index, (same, other) in enumerate(zip(near_slots, other_slots)):
        found[far[index]] = jnp.where(first, same[...], other[...])
        found[far[index + count // 2]] = jnp.where(first, other[...], same[...])
    slots = jnp.concatenate(
        [ref[:, ref.shape[1] - 128 :] for ref in near_refs] + [found[k] for k in sorted(far)]
    )
    for pick in range(hold_ref.shape[0]):
        found = lax.dot_general(
            slots, hold_ref[pick], LEADING, preferred_element_type=jnp.float32
        )
        gates_ref[pick : pick + 1, :] = found[:1].astype(jnp.bfloat16)
    width = handed_ref.shape[1]
    rows = jnp.concatenate([ref[...] for ref in row_refs])
    gated = message_ref[:, width:]
    handed = message_ref[:, :width].astype(jnp.float32) + matmul(gated, rows)
    later = lax.axis_index("section") < lax.axis_size("section") - 1
    handed_ref[...] = jnp.where(later, handed, 0.0).astype(jnp.bfloat16)


def layer(upstream, routes, gate_weights, w_gate, w_up, w_down, saved_gate, saved_up):
    grads_here = upstream[0]
    route_block = routes[0]
    parts = lax.axis_size("dp")
    experts = lax.axis_size("expert")
    capacity = saved_gate.shape[3]
    tokens, picks = route_block.shape
    width = grads_here.shape[1]
    units = w_down.shape[2]
    bf16 = lambda *shape: jax.ShapeDtypeStruct(shape, jnp.bfloat16)

    *rows, gated, holds = kernel_call(
        functools.partial(table_kernel, capacity, experts),
        (
            *[bf16(capacity, width)] * experts,
            bf16(experts * capacity, tokens),
            bf16(picks, experts * capacity, tokens),
        ),
        (route_block.T, gate_weights[0].T, grads_here),
        2 * experts * capacity * tokens * width,
        [pltpu.HBM] * 3,
        (
            pltpu.VMEM((picks, tokens), jnp.int32),
            pltpu.VMEM((picks, tokens), jnp.bfloat16),
            pltpu.VMEM((tokens, width), jnp.bfloat16),
            pltpu.SemaphoreType.DMA((3,)),
        ),
    )

    sections = lax.axis_size("section")

    def across(k, shift=0):
        return lambda s, d, e: ((s - shift) % sections, d, e ^ k)

    half = experts // 2
    far = list(range(experts - 1, half - 1, -1))
    cut = (len(far) + 1) // 2
    chunks = {"a": far[:cut], "b": far[cut:], "c": list(range(half))}
    arrived = {0: rows[0]}
    for name in ("a", "b", "c"):
        for k in chunks[name]:
            if k:
                arrived[k] = moved(rows[k], across(k))

    gate, up, gate_pre, up_pre = (w_gate[0, 0], w_up[0, 0], saved_gate[0, 0], saved_up[0, 0])
    down = kernel_call(
        fetch_kernel,
        bf16(units, width),
        (w_down[0, 0],),
        0,
        [pltpu.HBM],
        (pltpu.SemaphoreType.DMA,),
    )
    row_grad, slot_grad = ({}, {})
    for name in ("c", "a", "b"):
        chosen = chunks[name]
        count = len(chosen) * capacity
        total = kernel_call(
            raw_kernel,
            bf16(count, units),
            (*[arrived[k] for k in chosen], down),
            2 * count * width * units,
        )
        distance = 1
        while distance < parts:
            other = moved(total, lambda s, d, e, b=distance: (s, d ^ b, e))
            distance *= 2
            if distance < parts:
                total = (total.astype(jnp.float32) + other.astype(jnp.float32)).astype(jnp.bfloat16)
        outs = []
        for k in chosen:
            if name == "c" and k:
                outs.append(bf16(capacity, width + 128))
            else:
                outs.extend([bf16(capacity, width), bf16(capacity, 128)])
        results = list(
            kernel_call(
                functools.partial(back_kernel, tuple(chosen), capacity, name),
                tuple(outs),
                (total, other, gate_pre, up_pre, gate, up)
                + (tuple(slot_grad[k] for k in chunks["a"]) if name == "b" else ()),
                4 * count * width * units,
            )
        )
        for k in chosen:
            row_grad[k] = results.pop(0)
            if not (name == "c" and k):
                slot_grad[k] = results.pop(0)

    returned = {}
    for name in ("a", "b", "c"):
        for k in chunks[name]:
            if k:
                returned[k] = moved(row_grad[k], across(k, 0 if name == "c" else 1))
    message = kernel_call(
        partial_kernel,
        bf16(tokens, width + half * capacity),
        (grads_here, gated, row_grad[0], *[returned[k] for k in range(1, half)]),
        2 * tokens * width * half * capacity,
    )
    message = moved(message, across(0, 1))
    slot_back = [slot_grad[0], *[returned[k] for k in range(1, half)]]
    mine = []
    for first, second in zip(chunks["a"], chunks["b"]):
        mine.append(
            moved(
                slot_grad[second],
                lambda s, d, e, k=(first, second): (s, d, e ^ k[d & 1]),
            )
        )
    slot_back += mine + [moved(value, lambda s, d, e: (s, d ^ 1, e)) for value in mine]
    handed, gate_grads = kernel_call(
        functools.partial(finish_kernel, tuple(far)),
        (bf16(tokens, width), bf16(picks, tokens)),
        (message, holds, *[returned[k] for k in sorted(far)], *slot_back),
        2 * tokens * width * half * capacity,
    )
    return (handed[None], gate_grads.T[None])


def solution(mesh):
    placed = (
        P("section", "expert", "dp"),
        P("section", "expert", None),
        P("section", "expert", None),
        P("section", "expert", "dp", None),
        P("section", "expert", "dp", None),
        P("section", "expert", None, "dp"),
        P("section", "expert", None, None, None),
        P("section", "expert", None, None, None),
    )
    return jax.shard_map(
        layer,
        mesh=mesh,
        in_specs=placed,
        out_specs=(P("section", "expert", "dp"), P("section", "expert", None)),
        check_vma=False,
    )
```

```python
import functools

import jax
import jax.numpy as jnp
from jax import lax
from jax.experimental import pallas as pl
from jax.experimental.pallas import tpu as pltpu
from jax.sharding import PartitionSpec as P


AXES = ("section", "dp", "expert")
TRANSPOSED = (((1,), (1,)), ((), ()))
LEADING = (((0,), (0,)), ((), ()))


def device_pairs(route):
    sections, parts, experts = (lax.axis_size(name) for name in AXES)
    pairs = []
    for section in range(sections):
        for part in range(parts):
            for expert in range(experts):
                target = route(section, part, expert)
                if target is not None:
                    source_id = (section * parts + part) * experts + expert
                    target_id = (target[0] * parts + target[1]) * experts + target[2]
                    pairs.append((source_id, target_id))
    return pairs


def moved(value, route):
    return lax.ppermute(value, AXES, device_pairs(route))


def matmul(lhs, rhs):
    return jnp.dot(lhs, rhs, preferred_element_type=jnp.float32)


def matmul_t(lhs, rhs):
    return lax.dot_general(lhs, rhs, TRANSPOSED, preferred_element_type=jnp.float32)


def kernel_call(body, outs, ins, flops=0, spaces=None, scratch=()):
    spaces = spaces or [pltpu.VMEM] * len(ins)
    ins = [
        pltpu.with_memory_space_constraint(value, space) if space == pltpu.HBM else value
        for value, space in zip(ins, spaces)
    ]
    size = sum(value.size * value.dtype.itemsize for value in ins)
    return pl.pallas_call(
        body,
        out_shape=outs,
        in_specs=[pl.BlockSpec(memory_space=space) for space in spaces],
        out_specs=jax.tree.map(lambda _: pl.BlockSpec(memory_space=pltpu.VMEM), outs),
        scratch_shapes=scratch,
        compiler_params=pltpu.CompilerParams(vmem_limit_bytes=16 * 2**20),
        cost_estimate=pl.CostEstimate(flops=flops, bytes_accessed=size, transcendentals=0),
    )(*ins)


def slot_tables(capacity, experts, route_ref):
    picks, tokens = route_ref.shape
    slots = experts * capacity
    place = lax.broadcasted_iota(jnp.int32, (slots, 1), 0)
    block = lax.div(place, capacity)
    inside = (place - block * capacity).astype(jnp.float32)
    label = lax.axis_index("expert") ^ block
    row = lax.broadcasted_iota(jnp.int32, (tokens, tokens), 0)
    column = lax.broadcasted_iota(jnp.int32, (tokens, tokens), 1)
    before = jnp.where(row < column, 1.0, 0.0).astype(jnp.bfloat16)
    named = [route_ref[pick : pick + 1, :] == label for pick in range(picks)]
    names = functools.reduce(jnp.logical_or, named)
    earlier = matmul(jnp.where(names, 1.0, 0.0).astype(jnp.bfloat16), before)
    return named, names, earlier == inside


def copy_all(sources, targets, semaphores):
    copies = [
        pltpu.make_async_copy(source, target, semaphores.at[index])
        for index, (source, target) in enumerate(zip(sources, targets))
    ]
    for copy in copies:
        copy.start()
    return copies


def table_kernel(capacity, experts, route_hbm, grads_hbm, *refs):
    row_refs, (route_ref, grads_ref, semaphores) = (refs[:experts], refs[experts:])
    copies = copy_all((route_hbm, grads_hbm), (route_ref, grads_ref), semaphores)
    copies[0].wait()
    _, names, fits = slot_tables(capacity, experts, route_ref)
    placed = jnp.where(names & fits, 1.0, 0.0).astype(jnp.bfloat16)
    copies[1].wait()
    width = grads_ref.shape[1]
    tile = 256 if width % 256 == 0 else width
    for start in range(0, width, tile):
        part = pl.ds(start, tile)
        rows = matmul(placed, grads_ref[:, part]).astype(jnp.bfloat16)
        for k, ref in enumerate(row_refs):
            ref[:, part] = rows[k * capacity : (k + 1) * capacity]


def fetch_kernel(capacity, experts, route_hbm, gate_hbm, down_hbm, gated_ref, hold_ref, down_ref, route_ref, gate_ref, semaphores):
    copies = copy_all(
        (route_hbm, gate_hbm, down_hbm), (route_ref, gate_ref, down_ref), semaphores
    )
    picks, tokens = route_ref.shape
    copies[0].wait()
    named, _, fits = slot_tables(capacity, experts, route_ref)
    copies[1].wait()
    gated = jnp.zeros((experts * capacity, tokens), jnp.float32)
    for pick in range(picks):
        here = jnp.where(named[pick] & fits, 1.0, 0.0)
        hold_ref[pick] = here.astype(jnp.bfloat16)
        gated = gated + here * gate_ref[pick : pick + 1, :].astype(jnp.float32)
    gated_ref[...] = gated.astype(jnp.bfloat16)
    copies[2].wait()


def raw_kernel(*refs):
    row_refs, down_ref, out_ref = (refs[:-2], refs[-2], refs[-1])
    rows = jnp.concatenate([ref[...] for ref in row_refs])
    out_ref[...] = matmul_t(rows, down_ref[...]).astype(jnp.bfloat16)


def back_kernel(offsets, capacity, name, here_ref, other_ref, saved_gate_ref, saved_up_ref, gate_ref, up_ref, *refs):
    units = here_ref.shape[1]
    step = 256 if units % 256 == 0 else units
    inner, back = (0.0, 0.0)
    for start in range(0, units, step):
        part = pl.ds(start, step)
        total = here_ref[:, part].astype(jnp.float32) + other_ref[:, part].astype(jnp.float32)

        def picked(ref):
            return jnp.concatenate(
                [ref[lax.axis_index("expert") ^ k, :, part] for k in offsets]
            ).astype(jnp.float32)

        gate_val, up_val = (picked(saved_gate_ref), picked(saved_up_ref))
        sigmoid_val = jax.nn.sigmoid(gate_val)
        silu_val = gate_val * sigmoid_val
        hidden = (silu_val * up_val).astype(jnp.bfloat16).astype(jnp.float32)
        inner = inner + jnp.sum(hidden * total, axis=1, keepdims=True)
        gate_back = (
            total * up_val * sigmoid_val * (1.0 + gate_val * (1.0 - sigmoid_val))
        ).astype(jnp.bfloat16)
        up_back = (total * silu_val).astype(jnp.bfloat16)
        back = back + matmul_t(gate_back, gate_ref[:, part]) + matmul_t(up_back, up_ref[:, part])
    back = back.astype(jnp.bfloat16)
    inner = jnp.broadcast_to(inner, (inner.shape[0], 128)).astype(jnp.bfloat16)
    count = len(offsets)
    if name == "b":
        earlier, refs = (refs[:count], refs[count:])
        first = (lax.axis_index("dp") & 1) == 0
    outs = iter(refs)
    for index, k in enumerate(offsets):
        own = slice(index * capacity, (index + 1) * capacity)
        if name == "c" and k:
            joined = next(outs)
            joined[:, : back.shape[1]] = back[own]
            joined[:, back.shape[1] :] = inner[own]
        else:
            next(outs)[...] = back[own]
            next(outs)[...] = (
                jnp.where(first, earlier[index][...], inner[own]) if name == "b" else inner[own]
            )


def partial_kernel(grads_ref, gated_ref, first_ref, *refs):
    row_refs, message_ref = (refs[:-1], refs[-1])
    tokens, width = grads_ref.shape
    rows = jnp.concatenate([first_ref[...]] + [ref[:, :width] for ref in row_refs])
    near = rows.shape[0]
    partial = grads_ref[...].astype(jnp.float32) + lax.dot_general(
        gated_ref[:near], rows, LEADING, preferred_element_type=jnp.float32
    )
    message_ref[:, :width] = partial.astype(jnp.bfloat16)
    row = lax.broadcasted_iota(jnp.int32, (tokens, tokens), 0)
    column = lax.broadcasted_iota(jnp.int32, (tokens, tokens), 1)
    same = jnp.where(row == column, 1.0, 0.0).astype(jnp.bfloat16)
    message_ref[:, width:] = matmul_t(same, gated_ref[near:]).astype(jnp.bfloat16)


def finish_kernel(far, message_ref, hold_ref, *refs):
    count = len(far)
    row_refs, slot_refs, (handed_ref, gates_ref) = (refs[:count], refs[count:-2], refs[-2:])
    near_refs, near_slots, other_slots = (
        slot_refs[:-count],
        slot_refs[-count : -(count // 2)],
        slot_refs[-(count // 2) :],
    )
    first = (lax.axis_index("dp") & 1) == 0
    found = {}
    for index, (same, other) in enumerate(zip(near_slots, other_slots)):
        found[far[index]] = jnp.where(first, same[...], other[...])
        found[far[index + count // 2]] = jnp.where(first, other[...], same[...])
    slots = jnp.concatenate(
        [ref[:, ref.shape[1] - 128 :] for ref in near_refs] + [found[k] for k in sorted(far)]
    )
    for pick in range(hold_ref.shape[0]):
        found = lax.dot_general(
            slots, hold_ref[pick], LEADING, preferred_element_type=jnp.float32
        )
        gates_ref[pick : pick + 1, :] = found[:1].astype(jnp.bfloat16)
    width = handed_ref.shape[1]
    rows = jnp.concatenate([ref[...] for ref in row_refs])
    gated = message_ref[:, width:]
    handed = message_ref[:, :width].astype(jnp.float32) + matmul(gated, rows)
    later = lax.axis_index("section") < lax.axis_size("section") - 1
    handed_ref[...] = jnp.where(later, handed, 0.0).astype(jnp.bfloat16)


def layer(upstream, routes, gate_weights, w_gate, w_up, w_down, saved_gate, saved_up):
    grads_here = upstream[0]
    route_block = routes[0]
    parts = lax.axis_size("dp")
    experts = lax.axis_size("expert")
    capacity = saved_gate.shape[3]
    tokens, picks = route_block.shape
    width = grads_here.shape[1]
    units = w_down.shape[2]
    bf16 = lambda *shape: jax.ShapeDtypeStruct(shape, jnp.bfloat16)

    rows = kernel_call(
        functools.partial(table_kernel, capacity, experts),
        (bf16(capacity, width),) * experts,
        (route_block.T, grads_here),
        2 * experts * capacity * tokens * width,
        [pltpu.HBM] * 2,
        (
            pltpu.VMEM((picks, tokens), jnp.int32),
            pltpu.VMEM((tokens, width), jnp.bfloat16),
            pltpu.SemaphoreType.DMA((2,)),
        ),
    )

    sections = lax.axis_size("section")

    def across(k, shift=0):
        return lambda s, d, e: ((s - shift) % sections, d, e ^ k)

    half = experts // 2
    far = list(range(experts - 1, half - 1, -1))
    cut = (len(far) + 1) // 2
    chunks = {"a": far[:cut], "b": far[cut:], "c": list(range(half))}
    arrived = {0: rows[0]}
    for name in ("a", "b", "c"):
        for k in chunks[name]:
            if k:
                arrived[k] = moved(rows[k], across(k))

    gate, up, gate_pre, up_pre = (w_gate[0, 0], w_up[0, 0], saved_gate[0, 0], saved_up[0, 0])
    gated, holds, down = kernel_call(
        functools.partial(fetch_kernel, capacity, experts),
        (
            bf16(experts * capacity, tokens),
            bf16(picks, experts * capacity, tokens),
            bf16(units, width),
        ),
        (route_block.T, gate_weights[0].T, w_down[0, 0]),
        0,
        [pltpu.HBM] * 3,
        (
            pltpu.VMEM((picks, tokens), jnp.int32),
            pltpu.VMEM((picks, tokens), jnp.bfloat16),
            pltpu.SemaphoreType.DMA((3,)),
        ),
    )
    row_grad, slot_grad = ({}, {})
    for name in ("c", "a", "b"):
        chosen = chunks[name]
        count = len(chosen) * capacity
        total = kernel_call(
            raw_kernel,
            bf16(count, units),
            (*[arrived[k] for k in chosen], down),
            2 * count * width * units,
        )
        distance = 1
        while distance < parts:
            other = moved(total, lambda s, d, e, b=distance: (s, d ^ b, e))
            distance *= 2
            if distance < parts:
                total = (total.astype(jnp.float32) + other.astype(jnp.float32)).astype(jnp.bfloat16)
        outs = []
        for k in chosen:
            if name == "c" and k:
                outs.append(bf16(capacity, width + 128))
            else:
                outs.extend([bf16(capacity, width), bf16(capacity, 128)])
        results = list(
            kernel_call(
                functools.partial(back_kernel, tuple(chosen), capacity, name),
                tuple(outs),
                (total, other, gate_pre, up_pre, gate, up)
                + (tuple(slot_grad[k] for k in chunks["a"]) if name == "b" else ()),
                4 * count * width * units,
            )
        )
        for k in chosen:
            row_grad[k] = results.pop(0)
            if not (name == "c" and k):
                slot_grad[k] = results.pop(0)

    returned = {}
    for name in ("a", "b", "c"):
        for k in chunks[name]:
            if k:
                returned[k] = moved(row_grad[k], across(k, 0 if name == "c" else 1))
    message = kernel_call(
        partial_kernel,
        bf16(tokens, width + half * capacity),
        (grads_here, gated, row_grad[0], *[returned[k] for k in range(1, half)]),
        2 * tokens * width * half * capacity,
    )
    message = moved(message, across(0, 1))
    slot_back = [slot_grad[0], *[returned[k] for k in range(1, half)]]
    mine = []
    for first, second in zip(chunks["a"], chunks["b"]):
        mine.append(
            moved(
                slot_grad[second],
                lambda s, d, e, k=(first, second): (s, d, e ^ k[d & 1]),
            )
        )
    slot_back += mine + [moved(value, lambda s, d, e: (s, d ^ 1, e)) for value in mine]
    handed, gate_grads = kernel_call(
        functools.partial(finish_kernel, tuple(far)),
        (bf16(tokens, width), bf16(picks, tokens)),
        (message, holds, *[returned[k] for k in sorted(far)], *slot_back),
        2 * tokens * width * half * capacity,
    )
    return (handed[None], gate_grads.T[None])


def solution(mesh):
    placed = (
        P("section", "expert", "dp"),
        P("section", "expert", None),
        P("section", "expert", None),
        P("section", "expert", "dp", None),
        P("section", "expert", "dp", None),
        P("section", "expert", None, "dp"),
        P("section", "expert", None, None, None),
        P("section", "expert", None, None, None),
    )
    return jax.shard_map(
        layer,
        mesh=mesh,
        in_specs=placed,
        out_specs=(P("section", "expert", "dp"), P("section", "expert", None)),
        check_vma=False,
    )
```
